32 devices in a mesh: gx: 2 (over x), gy: 4 (over z), gz: 4 (over y, core).
Axes of the slice: x: 2, y: 2, z: 4, core: 2. Of those that a mesh axis runs over, the one named last changes fastest.
Arguments:
- camera_tiles: bfloat16 [6, 256, 1024], P(None, ('gx', 'gy'), 'gz'), may hold values from 0.049804688 to 4
- slot_lines: int32 [6, 256], P(None, ('gx', 'gy')), may hold values from -1 to 127, as said below
- view_shifts: int32 [6], replicated, may hold values from -8 to 8, as said below
- psf_width: float32 [6], replicated, may hold values from 16 to 64
- background: float32 [6], replicated, may hold values from 0.1 to 1
Outputs:
- joined_volume: float32 [16, 64, 1024], P('gx', 'gy', 'gz')
- coarse_level: float32 [8, 32, 512], P('gx', ('gy', 'gz'))
The draws below stay inside these ranges and needn't reach their ends.
Inputs may be any that keep to these rules, and one draw needn't show every extreme that they name: `slot_lines`: each entry is -1 (an empty slot) or a line of the owner brick, numbered x-major over its 8 x 16 columns. The 32 slots of one source block are 8 buckets of 4 slots in owner order, owners numbered with y fastest; the live slots of a bucket come first, and any bucket may hold 0 to 4 live slots. In every view some owner receives a full bucket from every source block. Lists are the same for all z layers. `view_shifts`: in every draw some view has shift 8 and another -8.
All inputs are finite; a program needn't handle non-finite values.
Results may differ from the reference program's by a relative error of at most 0.002.
Values may be sent and summed in bfloat16 or wider, within the bound.
A program may use at most 64 MiB of HBM per device.

```python
import math
import jax
import jax.numpy as jnp
from jax import lax

VIEWS = 6
PSF_REACH = 64
SHIFT_MAX = 8
HALO = 72
CX = 8
CY = 16
CAPACITY = 4
OWNERS = 8
SLOTS_DEV = 32
NZ = 1024
N_GX = 2
N_GY = 4


def draw_slot_lines(key, part):
    base_key = jax.random.fold_in(key, 11)
    live_key, hot_key, line_key = jax.random.split(base_key, 3)
    live_count = jax.random.randint(live_key, (VIEWS, OWNERS, OWNERS, 1), 0, CAPACITY + 1)
    hot_owner = jax.random.randint(hot_key, (VIEWS, 1, 1, 1), 0, OWNERS)
    owner_ids = jnp.arange(OWNERS, dtype=jnp.int32)[None, None, :, None]
    live_count = jnp.where(owner_ids == hot_owner, CAPACITY, live_count)
    slot_ids = jnp.arange(CAPACITY, dtype=jnp.int32)[None, None, None, :]
    line_ids = jax.random.randint(line_key, (VIEWS, OWNERS, OWNERS, CAPACITY), 0, CX * CY)
    chosen = jnp.where(slot_ids < live_count, line_ids, -1)
    return chosen.reshape(VIEWS, OWNERS * OWNERS * CAPACITY).astype(jnp.int32)


def draw_view_shifts(key, part):
    base_key = jax.random.fold_in(key, 23)
    value_key, order_key = jax.random.split(base_key, 2)
    shift_values = jax.random.randint(value_key, (VIEWS,), -SHIFT_MAX, SHIFT_MAX + 1)
    ordering = jax.random.permutation(order_key, VIEWS)
    view_ids = jnp.arange(VIEWS, dtype=jnp.int32)
    shift_values = jnp.where(view_ids == ordering[0], SHIFT_MAX, shift_values)
    shift_values = jnp.where(view_ids == ordering[1], -SHIFT_MAX, shift_values)
    return shift_values.astype(jnp.int32)


def level_of(key, dims, shards, smallest, high):
    level, own = 1.0, jax.random.fold_in(key, 6)
    for position, blocks in shards:
        draws = jnp.exp(jax.random.uniform(jax.random.fold_in(own, position), (blocks,), jnp.float32, smallest / len(shards), high / len(shards)))
        level = level * jnp.repeat(draws, dims[position] // blocks).reshape([-1 if axis == position else 1 for axis in range(len(dims))])
    return level


def setup_inputs(seed: int = 0) -> dict:
    arg_keys = jax.random.split(jax.random.key(seed), 6)
    camera_tiles = jnp.clip(jnp.exp(math.log(4.0) - 4.3859405 * jax.random.uniform(arg_keys[0], (VIEWS, OWNERS * SLOTS_DEV, NZ), jnp.float32) ** level_of(arg_keys[0], (VIEWS, OWNERS * SLOTS_DEV, NZ), ((1, 8), (2, 4)), -0.2, 0.2)), 0.049804688, 4.0).astype(jnp.bfloat16)
    slot_lines = draw_slot_lines(jax.random.fold_in(arg_keys[5], 71), 0)
    view_shifts = draw_view_shifts(jax.random.fold_in(arg_keys[5], 71), 0)
    psf_width = jnp.clip(jnp.exp(jax.random.uniform(arg_keys[3], (VIEWS,), jnp.float32, math.log(16.0), math.log(64.0))), 16.0, 64.0)
    background = jnp.clip(jnp.exp(jax.random.uniform(arg_keys[4], (VIEWS,), jnp.float32, math.log(0.1), math.log(1.0))), 0.1, 1.0)
    return dict(camera_tiles=camera_tiles, slot_lines=slot_lines, view_shifts=view_shifts, psf_width=psf_width, background=background)


def spread(offset, psf_width):
    taps = jnp.arange(-PSF_REACH, PSF_REACH + 1).astype(jnp.float32)
    total = jnp.sum(jnp.exp(-0.5 * (taps[None, :] / psf_width[:, None]) ** 2), axis=1)
    shaped_width = psf_width.reshape((-1,) + (1,) * (offset.ndim - 1))
    shaped_total = total.reshape((-1,) + (1,) * (offset.ndim - 1))
    inside = jnp.abs(offset) <= PSF_REACH
    values = jnp.where(inside, jnp.exp(-0.5 * (offset / shaped_width) ** 2), 0.0)
    return values / shaped_total


def decimate(volume, along_axis):
    half_length = (volume.shape[along_axis] - 2) // 2
    pieces = [lax.slice_in_dim(volume, first_index, first_index + 2 * half_length - 1, 2, along_axis) for first_index in range(4)]
    return (pieces[0] + 3.0 * pieces[1] + 3.0 * pieces[2] + pieces[3]) / 8.0


def reference(camera_tiles, slot_lines, view_shifts, psf_width, background):
    width_x = CX * N_GX
    width_y = CY * N_GY
    depth = camera_tiles.shape[2]
    slot_index = jnp.arange(camera_tiles.shape[1], dtype=jnp.int32)
    owner_index = (slot_index % SLOTS_DEV) // CAPACITY
    period = depth + 2 * HALO
    signed_index = jnp.arange(period, dtype=jnp.int32)
    signed_index = jnp.where(signed_index <= period // 2, signed_index, signed_index - period)
    offsets = (signed_index[None, :] - view_shifts[:, None]).astype(jnp.float32)
    kernels = spread(offsets, psf_width)
    kernel_freq = jnp.fft.rfft(kernels, axis=1)
    view_list = []
    for view_index in range(VIEWS):
        line_ids = slot_lines[view_index]
        x_global = (owner_index // N_GY) * CX + line_ids // CY
        y_global = (owner_index % N_GY) * CY + line_ids % CY
        target = jnp.where(line_ids >= 0, x_global * width_y + y_global, width_x * width_y).astype(jnp.int32)
        summed = jax.ops.segment_sum(camera_tiles[view_index].astype(jnp.float32), target, num_segments=width_x * width_y + 1)
        view_list.append(summed[: width_x * width_y])
    total_data = view_list[0]
    for view_index in range(1, VIEWS):
        total_data = total_data + view_list[view_index]
    estimate = total_data / VIEWS
    estimate_freq = jnp.fft.rfft(estimate, n=period, axis=1)
    total_correction = jnp.zeros_like(estimate)
    for view_index in range(VIEWS):
        blurred = jnp.fft.irfft(estimate_freq * kernel_freq[view_index][None, :], n=period, axis=1)[:, :depth]
        ratio = view_list[view_index] / (blurred + background[view_index])
        ratio_freq = jnp.fft.rfft(ratio, n=period, axis=1)
        correction = jnp.fft.irfft(ratio_freq * jnp.conj(kernel_freq[view_index])[None, :], n=period, axis=1)[:, :depth]
        total_correction = total_correction + correction
    joined = estimate * (total_correction / VIEWS)
    joined_volume = joined.reshape(width_x, width_y, depth)
    padded = jnp.pad(joined_volume, 1)
    coarse_level = decimate(decimate(decimate(padded, 2), 1), 0)
    return joined_volume, coarse_level
```

```python
import functools

import jax
import jax.numpy as jnp
from jax import lax
from jax.experimental import pallas as pl
from jax.experimental.pallas import tpu as pltpu
from jax.sharding import PartitionSpec as P

PSF_REACH = 64
CX = 8
CY = 16
CAPACITY = 4
ROWS = 32
LIST_ROW = 24
LANES = 128
MESH = pl.DeviceIdType.MESH


def iota(shape, dim):
    return lax.broadcasted_iota(jnp.int32, shape, dim)


def dot(a, b):
    return jnp.dot(a, b, preferred_element_type=jnp.float32)


def dot_split(a, b):
    high = a.astype(jnp.bfloat16)
    low = (a - high.astype(jnp.float32)).astype(jnp.bfloat16)
    return dot(high, b) + dot(low, b)


def tap(distance):
    weight = jnp.where((distance == 1) | (distance == 2), 3.0, 1.0)
    return jnp.where((distance >= 0) & (distance <= 3), weight, 0.0)


def spread_lanes(block, width):
    return jnp.concatenate([block] * (width // LANES), axis=1) if width > LANES else block


def kernel(
    n_gx, n_gy, n_gz, shifts_in, widths_in, backs_in, tiles_in, lists_in, joined_out, coarse_out,
    shifts, widths, backs, tiles, lists, local_sem, thin, weights, members, send, got, halo, vd, vd_side, est_b, partial,
    ratio, blur_w, corr_w, parts, sums, send_sem, got_sem, pass_sem, halo_sem, part_sem, sum_sem,
):
    views, slots, depth = tiles_in.shape
    n = n_gx * n_gy
    blocks = depth // LANES
    lines = CX * CY
    rows_y = CY // 2 // n_gz
    rows_x = CX // 2
    gx, gy, gz = lax.axis_index("gx"), lax.axis_index("gy"), lax.axis_index("gz")
    me = gx * n_gy + gy
    group = n_gz + 2
    used = blocks * ROWS - (ROWS - LIST_ROW if n <= 32 else 0)
    last = (blocks - 1) * ROWS

    def owner(o):
        return (o // n_gy, o % n_gy, gz)

    def tile_copy(src, dst, target):
        return pltpu.make_async_remote_copy(
            src_ref=send.at[dst, :used], dst_ref=got.at[src, :used], send_sem=send_sem.at[dst],
            recv_sem=got_sem.at[src], device_id=target, device_id_type=MESH,
        )

    def halo_copy(buf, src, side, target):
        first = last if side == 0 else 0
        return pltpu.make_async_remote_copy(
            src_ref=buf.at[src, first : first + LIST_ROW], dst_ref=halo.at[side, src, :LIST_ROW],
            send_sem=pass_sem.at[side, src], recv_sem=halo_sem.at[side, src], device_id=target, device_id_type=MESH,
        )

    def part_copy(p, c, src_z, target):
        return pltpu.make_async_remote_copy(
            src_ref=parts.at[p], dst_ref=sums.at[c, src_z], send_sem=part_sem.at[p],
            recv_sem=sum_sem.at[c, src_z], device_id=target, device_id_type=MESH,
        )

    def in_x(x):
        return (x >= 0) & (x < n_gx)

    def in_y(y):
        return (y >= 0) & (y < n_gy)

    def part_sends(act):
        for dxi, dx in ((0, -1), (2, 1), (1, 0)):
            @pl.when(in_x(gx + dx))
            def _():
                @pl.when(in_y(gy + 1))
                def _():
                    act(dxi * group + n_gz, dxi * 3 + 2, (gx + dx, gy + 1, 0))

                @pl.when(in_y(gy - 1))
                def _():
                    act(dxi * group + n_gz + 1, dxi * 3, (gx + dx, gy - 1, n_gz - 1))

                for r in range(1 if dx == 0 else 0, n_gz):
                    k = (gz + r) % n_gz
                    act(dxi * group + k, dxi * 3 + 1, (gx + dx, gy, k))

    def part_sources(act):
        for dxi, dx in enumerate((-1, 0, 1)):
            @pl.when(in_x(gx - dx))
            def _():
                for r in range(1 if dx == 0 else 0, n_gz):
                    z = (gz + r) % n_gz
                    act(dxi * 3 + 1, z, (gx - dx, gy, z))

                @pl.when(in_y(gy - 1) & (gz == 0))
                def _():
                    for z in range(n_gz):
                        act(dxi * 3 + 2, z, (gx - dx, gy - 1, z))

                @pl.when(in_y(gy + 1) & (gz == n_gz - 1))
                def _():
                    for z in range(n_gz):
                        act(dxi * 3, z, (gx - dx, gy + 1, z))

    barrier = pltpu.get_barrier_semaphore()

    def greet(target):
        pl.semaphore_signal(barrier, inc=1, device_id=target, device_id_type=MESH)

    def greet_owner(i, carry):
        greet(owner((me + n - i) % n))
        return carry

    lax.fori_loop(1, n, greet_owner, 0)

    @pl.when(gz > 0)
    def _():
        greet((gx, gy, gz - 1))

    @pl.when(gz < n_gz - 1)
    def _():
        greet((gx, gy, gz + 1))

    part_sources(lambda c, z, source: greet(source))

    pairs = (
        (tiles_in, tiles), (lists_in, lists), (shifts_in, shifts), (widths_in, widths), (backs_in, backs),
    )
    take = [pltpu.make_async_copy(a, b, local_sem.at[i]) for i, (a, b) in enumerate(pairs)]
    for copy in take:
        copy.start()

    halo[:, :, LIST_ROW:] = jnp.zeros((2, n, ROWS - LIST_ROW, LANES), jnp.bfloat16)
    if used < blocks * ROWS:
        got[:, used:] = jnp.zeros((n, blocks * ROWS - used, LANES), jnp.bfloat16)

    @pl.when(gz == 0)
    def _():
        halo[0, :, :LIST_ROW] = jnp.zeros((n, LIST_ROW, LANES), jnp.bfloat16)

    @pl.when(gz == n_gz - 1)
    def _():
        halo[1, :, :LIST_ROW] = jnp.zeros((n, LIST_ROW, LANES), jnp.bfloat16)

    for copy in take:
        copy.wait()
    flat = tiles[...].reshape(views * slots, depth)
    listed = (lists[...] + 1).astype(jnp.float32).astype(jnp.bfloat16)
    batch = min(n, 8)
    list_block, list_row = me // 32, LIST_ROW + me // 4 % 8
    for first in range(0, n, batch):
        shape = (batch * ROWS, views * slots)
        row = iota(shape, 0)
        q = row & (ROWS - 1)
        o = first + row // ROWS
        wanted = (q // CAPACITY) * slots + o * CAPACITY + (q & (CAPACITY - 1))
        pick = (iota(shape, 1) == wanted) & (q < views * CAPACITY)
        packed = dot(pick.astype(jnp.float32).astype(jnp.bfloat16), flat)
        shape = (slots, batch * LANES)
        lane = iota(shape, 1)
        spot = (first + lane // LANES) * CAPACITY + (lane & (CAPACITY - 1))
        spread = dot(listed, (iota(shape, 0) == spot).astype(jnp.float32).astype(jnp.bfloat16))
        lane = iota(spread.shape, 1) & (LANES - 1)
        mine = (lane // CAPACITY) == (me % 4) * (ROWS // CAPACITY) + iota(spread.shape, 0)
        ids = jnp.sum(jnp.where(mine, spread, 0.0), axis=0, keepdims=True)
        for i in range(batch):
            for b in range(blocks):
                body = packed[i * ROWS : (i + 1) * ROWS, b * LANES : (b + 1) * LANES]
                listing = (iota(body.shape, 0) == list_row) & (list_block == b)
                body = body + jnp.where(listing, ids[:, i * LANES : (i + 1) * LANES], 0.0)
                send[first + i, b * ROWS : (b + 1) * ROWS] = body.astype(jnp.bfloat16)
    got[me, :used] = send[me, :used]

    step = (iota((LANES, LANES), 1) - iota((LANES, LANES), 0)).astype(jnp.float32)
    reach = iota((1, LANES), 1)
    span = views * LANES
    for b in range(blocks + 2):
        for d in range(blocks):
            if not 0 <= b - d <= 2:
                corr_w[b * span : (b + 1) * span, d * LANES : (d + 1) * LANES] = jnp.zeros((span, LANES), jnp.bfloat16)
    for v in range(views):
        shift = shifts[v].astype(jnp.float32)
        inv = 1.0 / jnp.full((1, LANES), widths[v], jnp.float32)
        curve = -0.5 * inv * inv
        far = reach.astype(jnp.float32)
        half = jnp.where((reach >= 1) & (reach <= PSF_REACH), jnp.exp(far * far * curve), 0.0)
        scale = 1.0 / (1.0 + 2.0 * jnp.sum(half, axis=1, keepdims=True))
        for m in range(3):
            for sign in (-1.0, 1.0):
                off = step - (m - 1.0) * LANES + sign * shift
                value = jnp.exp(off * off * curve) * scale
                value = jnp.where(jnp.abs(off) <= PSF_REACH, value, 0.0).astype(jnp.bfloat16)
                if sign < 0:
                    blur_w[m * LANES : (m + 1) * LANES, v * LANES : (v + 1) * LANES] = value
                    continue
                for d in range(blocks):
                    at = (d + m) * span + v * LANES
                    corr_w[at : at + LANES, d * LANES : (d + 1) * LANES] = value

    half_depth = depth // 2
    z = iota((depth, half_depth + LANES), 0)
    k = iota((depth, half_depth + LANES), 1)
    k = jnp.where(k == half_depth + LANES - 1, -1, k)
    thin[...] = tap(z - 2 * k + 1).astype(jnp.bfloat16)
    r = iota((8, lines), 0)
    column = iota((8, lines), 1)
    rows = []
    for dx in (-1, 0, 1):
        for t in range(group):
            dy, z_part = (0, t) if t < n_gz else ((1, 0) if t == n_gz else (-1, n_gz - 1))
            i = rows_x * dx + r // rows_y
            j = (CY // 2) * dy + rows_y * z_part + r % rows_y
            weight = tap(column // CY - 2 * i + 1) * tap(column % CY - 2 * j + 1)
            rows.append(jnp.where(r < rows_x * rows_y, weight, 0.0))
    weights[...] = jnp.concatenate(rows, axis=0).astype(jnp.bfloat16)

    count = n - 1
    count = count + jnp.where(gz > 0, 1, 0) + jnp.where(gz < n_gz - 1, 1, 0)
    for dx in (-1, 0, 1):
        per = n_gz - (1 if dx == 0 else 0)
        per = per + jnp.where(in_y(gy + 1), 1, 0) + jnp.where(in_y(gy - 1), 1, 0)
        count = count + jnp.where(in_x(gx + dx), per, 0)
    pl.semaphore_wait(barrier, count)

    def send_tile(i, carry):
        o = (me + i) % n
        tile_copy(me, o, owner(o)).start()
        return carry

    lax.fori_loop(1, n, send_tile, 0)

    def pass_on(buf, src):
        @pl.when(gz > 0)
        def _():
            halo_copy(buf, src, 1, (gx, gy, gz - 1)).start()

        @pl.when(gz < n_gz - 1)
        def _():
            halo_copy(buf, src, 0, (gx, gy, gz + 1)).start()

    pass_on(send, me)

    def take_tile(i, carry):
        src = (me + n - i) % n
        tile_copy(src, me, owner(src)).wait_recv()
        pass_on(got, src)
        return carry

    lax.fori_loop(1, n, take_tile, 0)

    total = None
    for b in range(blocks if used == blocks * ROWS else 1):
        at = b * ROWS + 16
        ids = got[0, at : at + 16].astype(jnp.float32)
        for src in range(1, n):
            ids = ids + got[src, at : at + 16].astype(jnp.float32)
        total = ids[8:] if total is None else jnp.concatenate([total, ids[8:]], axis=0)
    ids = total
    line = (iota((lines, batch * ROWS), 0) + 1).astype(jnp.float32)
    lane = iota((lines, batch * ROWS), 1)
    view = (lane // CAPACITY) & (ROWS // CAPACITY - 1)

    for first in range(0, n, batch):
        at = first // 4
        pieces = [ids[at + i : at + i + 1] for i in range(-(-batch // 4))]
        hit = jnp.concatenate(pieces, axis=1)[:, : batch * ROWS] == line
        for v in range(views):
            owned = jnp.where(hit & (view == v), 1.0, 0.0)
            members[first // batch, v * lines : (v + 1) * lines] = owned.astype(jnp.bfloat16)
        owned = jnp.where(hit & (view < views), 1.0, 0.0)
        members[first // batch, views * lines :] = owned.astype(jnp.bfloat16)

    def landed(rows, load):
        total = None
        for first in range(0, n, batch):
            term = dot(members[first // batch, rows], load(first))
            total = term if total is None else total + term
        return total

    every = slice(0, views * lines)
    merged = slice(views * lines, (views + 1) * lines)

    def own(first):
        return jnp.concatenate(
            [
                got[first : first + batch, b * ROWS : (b + 1) * ROWS].reshape(batch * ROWS, LANES)
                for b in range(blocks)
            ],
            axis=1,
        )

    def beside(first):
        return jnp.concatenate(
            [halo[side, first : first + batch].reshape(batch * ROWS, LANES) for side in range(2)], axis=1
        )

    est = landed(merged, own) / views
    est_b[...] = est.astype(jnp.bfloat16)
    vd[...] = landed(every, own)
    for b in range(blocks + 2):
        low, high = max(b - 1, 1), min(b + 2, blocks + 1)
        partial[:, b * span : (b + 1) * span] = dot(
            est_b[:, (low - 1) * LANES : (high - 1) * LANES],
            blur_w[(low - b + 1) * LANES : (high - b + 1) * LANES],
        )

    def ratio_of(b, blurred):
        for v in range(views):
            rows = slice(v * lines, (v + 1) * lines)
            if b == 0:
                data = vd_side[rows, :LANES]
            elif b == blocks + 1:
                data = vd_side[rows, LANES:]
            else:
                data = vd[rows, (b - 1) * LANES : b * LANES]
            value = data / (blurred[:, v * LANES : (v + 1) * LANES] + jnp.full((1, LANES), backs[v], jnp.float32))
            ratio[:, b * span + v * LANES : b * span + (v + 1) * LANES] = value.astype(jnp.bfloat16)

    for b in range(2, blocks):
        ratio_of(b, partial[:, b * span : (b + 1) * span])

    @pl.when(gz > 0)
    def _():
        for src in range(n):
            halo_copy(got, src, 0, (gx, gy, gz)).wait_recv()

    @pl.when(gz < n_gz - 1)
    def _():
        for src in range(n):
            halo_copy(got, src, 1, (gx, gy, gz)).wait_recv()

    side = (landed(merged, beside) / views).astype(jnp.bfloat16)
    vd_side[...] = landed(every, beside)
    for edge, near, m, column_block in ((0, 1, 0, 0), (blocks + 1, blocks, 2, 1)):
        here = side[:, column_block * LANES : (column_block + 1) * LANES]
        for b, w in ((edge, 1), (near, m)):
            blurred = partial[:, b * span : (b + 1) * span] + dot(here, blur_w[w * LANES : (w + 1) * LANES])
            if blocks == 1 and b == 1:
                partial[:, span : 2 * span] = blurred
            ratio_of(b, blurred)
    correction = dot(ratio[...], corr_w[...])
    joined = est * (correction / views)
    joined_out[...] = joined.reshape(CX, CY, depth)

    halved = dot_split(joined, thin[...]) * (1.0 / 8)
    high = halved.astype(jnp.bfloat16)
    low = (halved - high.astype(jnp.float32)).astype(jnp.bfloat16)
    shares = (dot(weights[...], high) + dot(weights[...], low)) * (1.0 / 64)
    parts[...] = shares.reshape(3 * group, 8, half_depth + LANES)
    part_sends(lambda p, c, target: part_copy(p, c, gz, target).start())
    sums[4, gz] = parts[group + gz]
    def sent_tile(i, carry):
        o = (me + i) % n
        tile_copy(me, o, owner(o)).wait_send()
        return carry

    lax.fori_loop(1, n, sent_tile, 0)

    @pl.when(gz > 0)
    def _():
        for src in range(n):
            halo_copy(got, src, 1, (gx, gy, gz)).wait_send()

    @pl.when(gz < n_gz - 1)
    def _():
        for src in range(n):
            halo_copy(got, src, 0, (gx, gy, gz)).wait_send()

    part_sources(lambda c, s, source: part_copy(0, c, s, source).wait_recv())
    totals = []
    for s in range(n_gz):
        total = sums[4, s]
        for dxi, dx in enumerate((-1, 0, 1)):
            for c, there in ((0, in_y(gy + 1) & (gz == n_gz - 1)), (1, gz >= 0), (2, in_y(gy - 1) & (gz == 0))):
                if dx == 0 and c == 1:
                    continue
                total = total + jnp.where(in_x(gx - dx) & there, sums[dxi * 3 + c, s], 0.0)
        totals.append(total)
    lane = iota((8, half_depth), 1)
    for s in range(n_gz):
        total = totals[s][:, :half_depth]
        if s > 0:
            after = totals[s - 1][:, half_depth : half_depth + LANES]
            total = total + jnp.where(lane == 0, spread_lanes(after, half_depth), 0.0)
        if s < n_gz - 1:
            before = totals[s + 1][:, half_depth : half_depth + LANES]
            total = total + jnp.where(lane == half_depth - 1, spread_lanes(before, half_depth), 0.0)
        for i in range(rows_x):
            coarse_out[i, :, s * half_depth : (s + 1) * half_depth] = total[i * rows_y : (i + 1) * rows_y]
    part_sends(lambda p, c, target: part_copy(p, c, gz, target).wait_send())


def hand_on(joined, coarse, joined_out, coarse_out, sem):
    pairs = ((joined, joined_out), (coarse, coarse_out))
    put = [pltpu.make_async_copy(a, b, sem.at[i]) for i, (a, b) in enumerate(pairs)]
    for copy in put:
        copy.start()
    for copy in put:
        copy.wait()


def on_device(n_gx, n_gy, n_gz, camera_tiles, slot_lines, view_shifts, psf_width, background):
    views, slots, depth = camera_tiles.shape
    n = n_gx * n_gy
    packets = 3 * (n_gz + 2)
    blocks = depth // LANES
    lines = CX * CY
    span = views * LANES
    vmem = pl.BlockSpec(memory_space=pltpu.VMEM)
    hbm = pl.BlockSpec(memory_space=pl.ANY)
    results = pl.pallas_call(
        functools.partial(kernel, n_gx, n_gy, n_gz),
        out_shape=(
            pltpu.VMEM((CX, CY, depth), jnp.float32),
            pltpu.VMEM((CX // 2, CY // 2 // n_gz, depth // 2 * n_gz), jnp.float32),
        ),
        in_specs=[hbm] * 5,
        out_specs=(vmem, vmem),
        scratch_shapes=[
            pltpu.SMEM((views,), jnp.int32),
            pltpu.SMEM((views,), jnp.float32),
            pltpu.SMEM((views,), jnp.float32),
            pltpu.VMEM((views, slots, depth), jnp.bfloat16),
            pltpu.VMEM((views, slots), jnp.int32),
            pltpu.SemaphoreType.DMA((5,)),
            pltpu.VMEM((depth, depth // 2 + LANES), jnp.bfloat16),
            pltpu.VMEM((packets * 8, lines), jnp.bfloat16),
            pltpu.VMEM((-(-n // 8), (views + 1) * lines, min(n, 8) * ROWS), jnp.bfloat16),
            pltpu.VMEM((n, blocks * ROWS, LANES), jnp.bfloat16),
            pltpu.VMEM((n, blocks * ROWS, LANES), jnp.bfloat16),
            pltpu.VMEM((2, n, ROWS, LANES), jnp.bfloat16),
            pltpu.VMEM((views * lines, depth), jnp.float32),
            pltpu.VMEM((views * lines, 2 * LANES), jnp.float32),
            pltpu.VMEM((lines, depth), jnp.bfloat16),
            pltpu.VMEM((lines, (blocks + 2) * span), jnp.float32),
            pltpu.VMEM((lines, (blocks + 2) * span), jnp.bfloat16),
            pltpu.VMEM((3 * LANES, span), jnp.bfloat16),
            pltpu.VMEM(((blocks + 2) * span, depth), jnp.bfloat16),
            pltpu.VMEM((packets, 8, depth // 2 + LANES), jnp.float32),
            pltpu.VMEM((9, n_gz, 8, depth // 2 + LANES), jnp.float32),
            pltpu.SemaphoreType.DMA((n,)),
            pltpu.SemaphoreType.DMA((n,)),
            pltpu.SemaphoreType.DMA((2, n)),
            pltpu.SemaphoreType.DMA((2, n)),
            pltpu.SemaphoreType.DMA((packets,)),
            pltpu.SemaphoreType.DMA((9, n_gz)),
        ],
        compiler_params=pltpu.CompilerParams(collective_id=0, has_side_effects=True),
    )(view_shifts, psf_width, background, camera_tiles, slot_lines)
    return pl.pallas_call(
        hand_on,
        out_shape=tuple(jax.ShapeDtypeStruct(r.shape, r.dtype) for r in results),
        in_specs=[vmem, vmem],
        out_specs=(hbm, hbm),
        scratch_shapes=[pltpu.SemaphoreType.DMA((2,))],
        compiler_params=pltpu.CompilerParams(has_side_effects=True),
    )(*[pltpu.with_memory_space_constraint(r, pltpu.VMEM) for r in results])


def solution(mesh):
    sizes = (mesh.shape["gx"], mesh.shape["gy"], mesh.shape["gz"])
    in_specs = (P(None, ("gx", "gy"), "gz"), P(None, ("gx", "gy")), P(), P(), P())
    out_specs = (P("gx", "gy", "gz"), P("gx", ("gy", "gz"), None))
    return jax.shard_map(
        functools.partial(on_device, *sizes), mesh=mesh, in_specs=in_specs, out_specs=out_specs,
        check_vma=False,
    )
```

```python
import functools

import jax
import jax.numpy as jnp
from jax import lax
from jax.experimental import pallas as pl
from jax.experimental.pallas import tpu as pltpu
from jax.sharding import PartitionSpec as P

PSF_REACH = 64
CX = 8
CY = 16
CAPACITY = 4
ROWS = 32
LIST_ROW = 24
LANES = 128
MESH = pl.DeviceIdType.MESH


def iota(shape, dim):
    return lax.broadcasted_iota(jnp.int32, shape, dim)


def dot(a, b):
    return jnp.dot(a, b, preferred_element_type=jnp.float32)


def dot_split(a, b):
    high = a.astype(jnp.bfloat16)
    low = (a - high.astype(jnp.float32)).astype(jnp.bfloat16)
    return dot(high, b) + dot(low, b)


def tap(distance):
    weight = jnp.where((distance == 1) | (distance == 2), 3.0, 1.0)
    return jnp.where((distance >= 0) & (distance <= 3), weight, 0.0)


def spread_lanes(block, width):
    return jnp.concatenate([block] * (width // LANES), axis=1) if width > LANES else block


def kernel(
    n_gx, n_gy, n_gz, shifts_in, widths_in, backs_in, tiles_in, lists_in, joined_out, coarse_out,
    shifts, widths, backs, tiles, lists, local_sem, thin, weights, members, send, got, mid, halo, vd, vd_side, est_b, partial,
    ratio, blur_w, corr_w, parts, sums, send_sem, got_sem, mid_sem, next_sem, pass_sem, halo_sem, part_sem, sum_sem, ready,
):
    views, slots, depth = tiles_in.shape
    n = n_gx * n_gy
    blocks = depth // LANES
    lines = CX * CY
    rows_y = CY // 2 // n_gz
    rows_x = CX // 2
    gx, gy, gz = lax.axis_index("gx"), lax.axis_index("gy"), lax.axis_index("gz")
    me = gx * n_gy + gy
    group = n_gz + 2
    used = blocks * ROWS - (ROWS - LIST_ROW if n <= 32 else 0)
    last = (blocks - 1) * ROWS

    def owner(o):
        return (o // n_gy, o % n_gy, gz)

    def tile_copy(src, dst, target):
        return pltpu.make_async_remote_copy(
            src_ref=send.at[dst, :used], dst_ref=got.at[src, :used], send_sem=send_sem.at[dst],
            recv_sem=got_sem.at[src], device_id=target, device_id_type=MESH,
        )

    def across_copy(src_x, dst_x, y, target):
        return pltpu.make_async_remote_copy(
            src_ref=send.at[dst_x * n_gy + y, :used], dst_ref=mid.at[src_x * n_gy + y, :used],
            send_sem=send_sem.at[dst_x * n_gy + y], recv_sem=mid_sem.at[src_x * n_gy + y], device_id=target,
            device_id_type=MESH,
        )

    def next_copy(src_x, y, target):
        return pltpu.make_async_remote_copy(
            src_ref=mid.at[src_x * n_gy + y, :used], dst_ref=got.at[src_x * n_gy + gy, :used],
            send_sem=next_sem.at[src_x * n_gy + y], recv_sem=got_sem.at[src_x * n_gy + gy], device_id=target,
            device_id_type=MESH,
        )

    def others_x(act):
        def one(i, carry):
            act((gx + i) % n_gx)
            return carry

        lax.fori_loop(1, n_gx, one, 0)

    def at_distance(d, act):
        for index, sign in ((0, 1), (1, -1)):
            @pl.when(in_y(gy + sign * d))
            def _():
                act(index, gy + sign * d)

    def halo_copy(buf, src, side, target):
        first = last if side == 0 else 0
        return pltpu.make_async_remote_copy(
            src_ref=buf.at[src, first : first + LIST_ROW], dst_ref=halo.at[side, src, :LIST_ROW],
            send_sem=pass_sem.at[side, src], recv_sem=halo_sem.at[side, src], device_id=target, device_id_type=MESH,
        )

    def part_copy(p, c, src_z, target):
        return pltpu.make_async_remote_copy(
            src_ref=parts.at[p], dst_ref=sums.at[c, src_z], send_sem=part_sem.at[p],
            recv_sem=sum_sem.at[c, src_z], device_id=target, device_id_type=MESH,
        )

    def in_x(x):
        return (x >= 0) & (x < n_gx)

    def in_y(y):
        return (y >= 0) & (y < n_gy)

    def part_sends(act):
        for dxi, dx in ((0, -1), (2, 1), (1, 0)):
            @pl.when(in_x(gx + dx))
            def _():
                @pl.when(in_y(gy + 1))
                def _():
                    act(dxi * group + n_gz, dxi * 3 + 2, (gx + dx, gy + 1, 0))

                @pl.when(in_y(gy - 1))
                def _():
                    act(dxi * group + n_gz + 1, dxi * 3, (gx + dx, gy - 1, n_gz - 1))

                for r in range(1 if dx == 0 else 0, n_gz):
                    k = (gz + r) % n_gz
                    act(dxi * group + k, dxi * 3 + 1, (gx + dx, gy, k))

    def part_sources(act):
        for dxi, dx in enumerate((-1, 0, 1)):
            @pl.when(in_x(gx - dx))
            def _():
                for r in range(1 if dx == 0 else 0, n_gz):
                    z = (gz + r) % n_gz
                    act(dxi * 3 + 1, z, (gx - dx, gy, z))

                @pl.when(in_y(gy - 1) & (gz == 0))
                def _():
                    for z in range(n_gz):
                        act(dxi * 3 + 2, z, (gx - dx, gy - 1, z))

                @pl.when(in_y(gy + 1) & (gz == n_gz - 1))
                def _():
                    for z in range(n_gz):
                        act(dxi * 3, z, (gx - dx, gy + 1, z))

    barrier = pltpu.get_barrier_semaphore()

    def greet(target):
        pl.semaphore_signal(barrier, inc=1, device_id=target, device_id_type=MESH)

    others_x(lambda x: greet((x, gy, gz)))
    at_distance(1, lambda index, y: greet((gx, y, gz)))
    for r in range(1, n_gz):
        greet((gx, gy, (gz + r) % n_gz))

    pairs = (
        (tiles_in, tiles), (lists_in, lists), (shifts_in, shifts), (widths_in, widths), (backs_in, backs),
    )
    take = [pltpu.make_async_copy(a, b, local_sem.at[i]) for i, (a, b) in enumerate(pairs)]
    for copy in take:
        copy.start()

    halo[:, :, LIST_ROW:] = jnp.zeros((2, n, ROWS - LIST_ROW, LANES), jnp.bfloat16)
    if used < blocks * ROWS:
        got[:, used:] = jnp.zeros((n, blocks * ROWS - used, LANES), jnp.bfloat16)

    @pl.when(gz == 0)
    def _():
        halo[0, :, :LIST_ROW] = jnp.zeros((n, LIST_ROW, LANES), jnp.bfloat16)

    @pl.when(gz == n_gz - 1)
    def _():
        halo[1, :, :LIST_ROW] = jnp.zeros((n, LIST_ROW, LANES), jnp.bfloat16)

    for copy in take:
        copy.wait()
    flat = tiles[...].reshape(views * slots, depth)
    listed = (lists[...] + 1).astype(jnp.float32).astype(jnp.bfloat16)
    batch = min(n, 8)
    list_block, list_row = me // 32, LIST_ROW + me // 4 % 8
    for first in range(0, n, batch):
        shape = (batch * ROWS, views * slots)
        row = iota(shape, 0)
        q = row & (ROWS - 1)
        o = first + row // ROWS
        wanted = (q // CAPACITY) * slots + o * CAPACITY + (q & (CAPACITY - 1))
        pick = (iota(shape, 1) == wanted) & (q < views * CAPACITY)
        packed = dot(pick.astype(jnp.float32).astype(jnp.bfloat16), flat)
        shape = (slots, batch * LANES)
        lane = iota(shape, 1)
        spot = (first + lane // LANES) * CAPACITY + (lane & (CAPACITY - 1))
        spread = dot(listed, (iota(shape, 0) == spot).astype(jnp.float32).astype(jnp.bfloat16))
        lane = iota(spread.shape, 1) & (LANES - 1)
        mine = (lane // CAPACITY) == (me % 4) * (ROWS // CAPACITY) + iota(spread.shape, 0)
        ids = jnp.sum(jnp.where(mine, spread, 0.0), axis=0, keepdims=True)
        for i in range(batch):
            for b in range(blocks):
                body = packed[i * ROWS : (i + 1) * ROWS, b * LANES : (b + 1) * LANES]
                listing = (iota(body.shape, 0) == list_row) & (list_block == b)
                body = body + jnp.where(listing, ids[:, i * LANES : (i + 1) * LANES], 0.0)
                send[first + i, b * ROWS : (b + 1) * ROWS] = body.astype(jnp.bfloat16)
    got[me, :used] = send[me, :used]

    count = n_gx - 1 + n_gz - 1 + jnp.where(in_y(gy + 1), 1, 0) + jnp.where(in_y(gy - 1), 1, 0)
    pl.semaphore_wait(barrier, count)

    def send_across(y):
        others_x(lambda x: across_copy(gx, x, y, (x, gy, gz)).start())

    def send_along(y):
        tile_copy(me, gx * n_gy + y, (gx, y, gz)).start()

    for d in range(n_gy - 1, 0, -1):
        at_distance(d, lambda index, y: send_across(y))
    others_x(lambda x: tile_copy(me, x * n_gy + gy, (x, gy, gz)).start())
    at_distance(1, lambda index, y: send_along(y))

    def pass_on(buf, src):
        @pl.when(gz > 0)
        def _():
            halo_copy(buf, src, 1, (gx, gy, gz - 1)).start()

        @pl.when(gz < n_gz - 1)
        def _():
            halo_copy(buf, src, 0, (gx, gy, gz + 1)).start()

    pass_on(send, me)

    for d in range(2, n_gy):
        for index, sign in ((0, 1), (1, -1)):
            @pl.when(in_y(gy + sign * (d - 1)) & in_y(gy - sign))
            def _():
                pl.semaphore_signal(
                    ready.at[index, d], inc=1, device_id=(gx, gy - sign, gz), device_id_type=MESH
                )

        def reach_out(index, y):
            pl.semaphore_wait(ready.at[index, d], 1)
            send_along(y)

        at_distance(d, reach_out)

    def hand_along(y):
        def one(x):
            across_copy(x, gx, y, (x, gy, gz)).wait_recv()
            next_copy(x, y, (gx, y, gz)).start()

        others_x(one)

    for d in range(n_gy - 1, 0, -1):
        at_distance(d, lambda index, y: hand_along(y))

    step = (iota((LANES, LANES), 1) - iota((LANES, LANES), 0)).astype(jnp.float32)
    reach = iota((1, LANES), 1)
    span = views * LANES
    for b in range(blocks + 2):
        for d in range(blocks):
            if not 0 <= b - d <= 2:
                corr_w[b * span : (b + 1) * span, d * LANES : (d + 1) * LANES] = jnp.zeros((span, LANES), jnp.bfloat16)
    for v in range(views):
        shift = shifts[v].astype(jnp.float32)
        inv = 1.0 / jnp.full((1, LANES), widths[v], jnp.float32)
        curve = -0.5 * inv * inv
        far = reach.astype(jnp.float32)
        half = jnp.where((reach >= 1) & (reach <= PSF_REACH), jnp.exp(far * far * curve), 0.0)
        scale = 1.0 / (1.0 + 2.0 * jnp.sum(half, axis=1, keepdims=True))
        for m in range(3):
            for sign in (-1.0, 1.0):
                off = step - (m - 1.0) * LANES + sign * shift
                value = jnp.exp(off * off * curve) * scale
                value = jnp.where(jnp.abs(off) <= PSF_REACH, value, 0.0).astype(jnp.bfloat16)
                if sign < 0:
                    blur_w[m * LANES : (m + 1) * LANES, v * LANES : (v + 1) * LANES] = value
                    continue
                for d in range(blocks):
                    at = (d + m) * span + v * LANES
                    corr_w[at : at + LANES, d * LANES : (d + 1) * LANES] = value

    half_depth = depth // 2
    z = iota((depth, half_depth + LANES), 0)
    k = iota((depth, half_depth + LANES), 1)
    k = jnp.where(k == half_depth + LANES - 1, -1, k)
    thin[...] = tap(z - 2 * k + 1).astype(jnp.bfloat16)
    r = iota((8, lines), 0)
    column = iota((8, lines), 1)
    rows = []
    for dx in (-1, 0, 1):
        for t in range(group):
            dy, z_part = (0, t) if t < n_gz else ((1, 0) if t == n_gz else (-1, n_gz - 1))
            i = rows_x * dx + r // rows_y
            j = (CY // 2) * dy + rows_y * z_part + r % rows_y
            weight = tap(column // CY - 2 * i + 1) * tap(column % CY - 2 * j + 1)
            rows.append(jnp.where(r < rows_x * rows_y, weight, 0.0))
    weights[...] = jnp.concatenate(rows, axis=0).astype(jnp.bfloat16)

    def take_tile(x, y):
        src = x * n_gy + y
        tile_copy(src, me, (x, y, gz)).wait_recv()
        pass_on(got, src)

    others_x(lambda x: take_tile(x, gy))

    def take_column(y):
        take_tile(gx, y)
        others_x(lambda x: take_tile(x, y))

    for d in range(1, n_gy):
        at_distance(d, lambda index, y: take_column(y))

    total = None
    for b in range(blocks if used == blocks * ROWS else 1):
        at = b * ROWS + 16
        ids = got[0, at : at + 16].astype(jnp.float32)
        for src in range(1, n):
            ids = ids + got[src, at : at + 16].astype(jnp.float32)
        total = ids[8:] if total is None else jnp.concatenate([total, ids[8:]], axis=0)
    ids = total
    line = (iota((lines, batch * ROWS), 0) + 1).astype(jnp.float32)
    lane = iota((lines, batch * ROWS), 1)
    view = (lane // CAPACITY) & (ROWS // CAPACITY - 1)

    for first in range(0, n, batch):
        at = first // 4
        pieces = [ids[at + i : at + i + 1] for i in range(-(-batch // 4))]
        hit = jnp.concatenate(pieces, axis=1)[:, : batch * ROWS] == line
        for v in range(views):
            owned = jnp.where(hit & (view == v), 1.0, 0.0)
            members[first // batch, v * lines : (v + 1) * lines] = owned.astype(jnp.bfloat16)
        owned = jnp.where(hit & (view < views), 1.0, 0.0)
        members[first // batch, views * lines :] = owned.astype(jnp.bfloat16)

    def landed(rows, load):
        total = None
        for first in range(0, n, batch):
            term = dot(members[first // batch, rows], load(first))
            total = term if total is None else total + term
        return total

    every = slice(0, views * lines)
    merged = slice(views * lines, (views + 1) * lines)

    def own(first):
        return jnp.concatenate(
            [
                got[first : first + batch, b * ROWS : (b + 1) * ROWS].reshape(batch * ROWS, LANES)
                for b in range(blocks)
            ],
            axis=1,
        )

    def beside(first):
        return jnp.concatenate(
            [halo[side, first : first + batch].reshape(batch * ROWS, LANES) for side in range(2)], axis=1
        )

    est = landed(merged, own) / views
    est_b[...] = est.astype(jnp.bfloat16)
    vd[...] = landed(every, own)
    for b in range(blocks + 2):
        low, high = max(b - 1, 1), min(b + 2, blocks + 1)
        partial[:, b * span : (b + 1) * span] = dot(
            est_b[:, (low - 1) * LANES : (high - 1) * LANES],
            blur_w[(low - b + 1) * LANES : (high - b + 1) * LANES],
        )

    def ratio_of(b, blurred):
        for v in range(views):
            rows = slice(v * lines, (v + 1) * lines)
            if b == 0:
                data = vd_side[rows, :LANES]
            elif b == blocks + 1:
                data = vd_side[rows, LANES:]
            else:
                data = vd[rows, (b - 1) * LANES : b * LANES]
            value = data / (blurred[:, v * LANES : (v + 1) * LANES] + jnp.full((1, LANES), backs[v], jnp.float32))
            ratio[:, b * span + v * LANES : b * span + (v + 1) * LANES] = value.astype(jnp.bfloat16)

    for b in range(2, blocks):
        ratio_of(b, partial[:, b * span : (b + 1) * span])

    @pl.when(gz > 0)
    def _():
        for src in range(n):
            halo_copy(got, src, 0, (gx, gy, gz)).wait_recv()

    @pl.when(gz < n_gz - 1)
    def _():
        for src in range(n):
            halo_copy(got, src, 1, (gx, gy, gz)).wait_recv()

    side = (landed(merged, beside) / views).astype(jnp.bfloat16)
    vd_side[...] = landed(every, beside)
    for edge, near, m, column_block in ((0, 1, 0, 0), (blocks + 1, blocks, 2, 1)):
        here = side[:, column_block * LANES : (column_block + 1) * LANES]
        for b, w in ((edge, 1), (near, m)):
            blurred = partial[:, b * span : (b + 1) * span] + dot(here, blur_w[w * LANES : (w + 1) * LANES])
            if blocks == 1 and b == 1:
                partial[:, span : 2 * span] = blurred
            ratio_of(b, blurred)
    correction = dot(ratio[...], corr_w[...])
    joined = est * (correction / views)
    joined_out[...] = joined.reshape(CX, CY, depth)

    halved = dot_split(joined, thin[...]) * (1.0 / 8)
    high = halved.astype(jnp.bfloat16)
    low = (halved - high.astype(jnp.float32)).astype(jnp.bfloat16)
    shares = (dot(weights[...], high) + dot(weights[...], low)) * (1.0 / 64)
    parts[...] = shares.reshape(3 * group, 8, half_depth + LANES)
    part_sends(lambda p, c, target: part_copy(p, c, gz, target).start())
    sums[4, gz] = parts[group + gz]
    def sent_tile(i, carry):
        o = (me + i) % n
        tile_copy(me, o, owner(o)).wait_send()
        return carry

    lax.fori_loop(1, n, sent_tile, 0)
    for d in range(1, n_gy):
        at_distance(d, lambda index, y: others_x(lambda x: next_copy(x, y, (gx, y, gz)).wait_send()))

    @pl.when(gz > 0)
    def _():
        for src in range(n):
            halo_copy(got, src, 1, (gx, gy, gz)).wait_send()

    @pl.when(gz < n_gz - 1)
    def _():
        for src in range(n):
            halo_copy(got, src, 0, (gx, gy, gz)).wait_send()

    part_sources(lambda c, s, source: part_copy(0, c, s, source).wait_recv())
    totals = []
    for s in range(n_gz):
        total = sums[4, s]
        for dxi, dx in enumerate((-1, 0, 1)):
            for c, there in ((0, in_y(gy + 1) & (gz == n_gz - 1)), (1, gz >= 0), (2, in_y(gy - 1) & (gz == 0))):
                if dx == 0 and c == 1:
                    continue
                total = total + jnp.where(in_x(gx - dx) & there, sums[dxi * 3 + c, s], 0.0)
        totals.append(total)
    lane = iota((8, half_depth), 1)
    for s in range(n_gz):
        total = totals[s][:, :half_depth]
        if s > 0:
            after = totals[s - 1][:, half_depth : half_depth + LANES]
            total = total + jnp.where(lane == 0, spread_lanes(after, half_depth), 0.0)
        if s < n_gz - 1:
            before = totals[s + 1][:, half_depth : half_depth + LANES]
            total = total + jnp.where(lane == half_depth - 1, spread_lanes(before, half_depth), 0.0)
        for i in range(rows_x):
            coarse_out[i, :, s * half_depth : (s + 1) * half_depth] = total[i * rows_y : (i + 1) * rows_y]
    part_sends(lambda p, c, target: part_copy(p, c, gz, target).wait_send())


def hand_on(joined, coarse, joined_out, coarse_out, sem):
    pairs = ((joined, joined_out), (coarse, coarse_out))
    put = [pltpu.make_async_copy(a, b, sem.at[i]) for i, (a, b) in enumerate(pairs)]
    for copy in put:
        copy.start()
    for copy in put:
        copy.wait()


def on_device(n_gx, n_gy, n_gz, camera_tiles, slot_lines, view_shifts, psf_width, background):
    views, slots, depth = camera_tiles.shape
    n = n_gx * n_gy
    packets = 3 * (n_gz + 2)
    blocks = depth // LANES
    lines = CX * CY
    span = views * LANES
    vmem = pl.BlockSpec(memory_space=pltpu.VMEM)
    hbm = pl.BlockSpec(memory_space=pl.ANY)
    results = pl.pallas_call(
        functools.partial(kernel, n_gx, n_gy, n_gz),
        out_shape=(
            pltpu.VMEM((CX, CY, depth), jnp.float32),
            pltpu.VMEM((CX // 2, CY // 2 // n_gz, depth // 2 * n_gz), jnp.float32),
        ),
        in_specs=[hbm] * 5,
        out_specs=(vmem, vmem),
        scratch_shapes=[
            pltpu.SMEM((views,), jnp.int32),
            pltpu.SMEM((views,), jnp.float32),
            pltpu.SMEM((views,), jnp.float32),
            pltpu.VMEM((views, slots, depth), jnp.bfloat16),
            pltpu.VMEM((views, slots), jnp.int32),
            pltpu.SemaphoreType.DMA((5,)),
            pltpu.VMEM((depth, depth // 2 + LANES), jnp.bfloat16),
            pltpu.VMEM((packets * 8, lines), jnp.bfloat16),
            pltpu.VMEM((-(-n // 8), (views + 1) * lines, min(n, 8) * ROWS), jnp.bfloat16),
            pltpu.VMEM((n, blocks * ROWS, LANES), jnp.bfloat16),
            pltpu.VMEM((n, blocks * ROWS, LANES), jnp.bfloat16),
            pltpu.VMEM((n, blocks * ROWS, LANES), jnp.bfloat16),
            pltpu.VMEM((2, n, ROWS, LANES), jnp.bfloat16),
            pltpu.VMEM((views * lines, depth), jnp.float32),
            pltpu.VMEM((views * lines, 2 * LANES), jnp.float32),
            pltpu.VMEM((lines, depth), jnp.bfloat16),
            pltpu.VMEM((lines, (blocks + 2) * span), jnp.float32),
            pltpu.VMEM((lines, (blocks + 2) * span), jnp.bfloat16),
            pltpu.VMEM((3 * LANES, span), jnp.bfloat16),
            pltpu.VMEM(((blocks + 2) * span, depth), jnp.bfloat16),
            pltpu.VMEM((packets, 8, depth // 2 + LANES), jnp.float32),
            pltpu.VMEM((9, n_gz, 8, depth // 2 + LANES), jnp.float32),
            pltpu.SemaphoreType.DMA((n,)),
            pltpu.SemaphoreType.DMA((n,)),
            pltpu.SemaphoreType.DMA((n,)),
            pltpu.SemaphoreType.DMA((n,)),
            pltpu.SemaphoreType.DMA((2, n)),
            pltpu.SemaphoreType.DMA((2, n)),
            pltpu.SemaphoreType.DMA((packets,)),
            pltpu.SemaphoreType.DMA((9, n_gz)),
            pltpu.SemaphoreType.REGULAR((2, n_gy)),
        ],
        compiler_params=pltpu.CompilerParams(collective_id=0, has_side_effects=True),
    )(view_shifts, psf_width, background, camera_tiles, slot_lines)
    return pl.pallas_call(
        hand_on,
        out_shape=tuple(jax.ShapeDtypeStruct(r.shape, r.dtype) for r in results),
        in_specs=[vmem, vmem],
        out_specs=(hbm, hbm),
        scratch_shapes=[pltpu.SemaphoreType.DMA((2,))],
        compiler_params=pltpu.CompilerParams(has_side_effects=True),
    )(*[pltpu.with_memory_space_constraint(r, pltpu.VMEM) for r in results])


def solution(mesh):
    sizes = (mesh.shape["gx"], mesh.shape["gy"], mesh.shape["gz"])
    in_specs = (P(None, ("gx", "gy"), "gz"), P(None, ("gx", "gy")), P(), P(), P())
    out_specs = (P("gx", "gy", "gz"), P("gx", ("gy", "gz"), None))
    return jax.shard_map(
        functools.partial(on_device, *sizes), mesh=mesh, in_specs=in_specs, out_specs=out_specs,
        check_vma=False,
    )
```

```python
import functools

import jax
import jax.numpy as jnp
from jax import lax
from jax.experimental import pallas as pl
from jax.experimental.pallas import tpu as pltpu
from jax.sharding import PartitionSpec as P

PSF_REACH = 64
CX = 8
CY = 16
CAPACITY = 4
ROWS = 32
LIST_ROW = 24
LANES = 128
MESH = pl.DeviceIdType.MESH


def iota(shape, dim):
    return lax.broadcasted_iota(jnp.int32, shape, dim)


def dot(a, b):
    return jnp.dot(a, b, preferred_element_type=jnp.float32)


def dot_split(a, b):
    high = a.astype(jnp.bfloat16)
    low = (a - high.astype(jnp.float32)).astype(jnp.bfloat16)
    return dot(high, b) + dot(low, b)


def tap(distance):
    weight = jnp.where((distance == 1) | (distance == 2), 3.0, 1.0)
    return jnp.where((distance >= 0) & (distance <= 3), weight, 0.0)


def spread_lanes(block, width):
    return jnp.concatenate([block] * (width // LANES), axis=1) if width > LANES else block


def kernel(
    n_gx, n_gy, n_gz, shifts_in, widths_in, backs_in, tiles_in, lists_in, joined_out, coarse_out,
    shifts, widths, backs, tiles, lists, local_sem, thin, weights, members, send, got, halo, vd, vd_side, est_b, partial,
    ratio, blur_w, corr_w, parts, edges, sums, edge_sums, send_sem, got_sem, pass_sem, halo_sem, part_sem, sum_sem,
):
    views, slots, depth = tiles_in.shape
    n = n_gx * n_gy
    blocks = depth // LANES
    lines = CX * CY
    rows_y = CY // 2 // n_gz
    rows_x = CX // 2
    gx, gy, gz = lax.axis_index("gx"), lax.axis_index("gy"), lax.axis_index("gz")
    me = gx * n_gy + gy
    group = n_gz + 2
    used = blocks * ROWS - (ROWS - LIST_ROW if n <= 32 else 0)
    last = (blocks - 1) * ROWS

    def owner(o):
        return (o // n_gy, o % n_gy, gz)

    def tile_copy(src, dst, target):
        return pltpu.make_async_remote_copy(
            src_ref=send.at[dst, :used], dst_ref=got.at[src, :used], send_sem=send_sem.at[dst],
            recv_sem=got_sem.at[src], device_id=target, device_id_type=MESH,
        )

    def halo_copy(buf, src, side, target):
        first = last if side == 0 else 0
        return pltpu.make_async_remote_copy(
            src_ref=buf.at[src, first : first + LIST_ROW], dst_ref=halo.at[side, src, :LIST_ROW],
            send_sem=pass_sem.at[side, src], recv_sem=halo_sem.at[side, src], device_id=target, device_id_type=MESH,
        )

    def part_copy(dxi, part, cy, src_z, target):
        if dxi == 1:
            src, dst = parts.at[part], sums.at[cy, src_z]
        else:
            src, dst = edges.at[dxi // 2, part], edge_sums.at[dxi // 2, cy, src_z]
        return pltpu.make_async_remote_copy(
            src_ref=src, dst_ref=dst, send_sem=part_sem.at[dxi * group + part],
            recv_sem=sum_sem.at[dxi * 3 + cy, src_z], device_id=target, device_id_type=MESH,
        )

    def in_x(x):
        return (x >= 0) & (x < n_gx)

    def in_y(y):
        return (y >= 0) & (y < n_gy)

    def part_sends(act):
        for dxi, dx in ((0, -1), (2, 1), (1, 0)):
            @pl.when(in_x(gx + dx))
            def _():
                @pl.when(in_y(gy + 1))
                def _():
                    act(dxi, n_gz, 2, (gx + dx, gy + 1, 0))

                @pl.when(in_y(gy - 1))
                def _():
                    act(dxi, n_gz + 1, 0, (gx + dx, gy - 1, n_gz - 1))

                for r in range(1 if dx == 0 else 0, n_gz):
                    k = (gz + r) % n_gz
                    act(dxi, k, 1, (gx + dx, gy, k))

    def part_sources(act):
        for dxi, dx in enumerate((-1, 0, 1)):
            @pl.when(in_x(gx - dx))
            def _():
                for r in range(1 if dx == 0 else 0, n_gz):
                    z = (gz + r) % n_gz
                    act(dxi, 1, z, (gx - dx, gy, z))

                @pl.when(in_y(gy - 1) & (gz == 0))
                def _():
                    for z in range(n_gz):
                        act(dxi, 2, z, (gx - dx, gy - 1, z))

                @pl.when(in_y(gy + 1) & (gz == n_gz - 1))
                def _():
                    for z in range(n_gz):
                        act(dxi, 0, z, (gx - dx, gy + 1, z))

    barrier = pltpu.get_barrier_semaphore()

    def greet(target):
        pl.semaphore_signal(barrier, inc=1, device_id=target, device_id_type=MESH)

    def greet_owner(i, carry):
        greet(owner((me + n - i) % n))
        return carry

    lax.fori_loop(1, n, greet_owner, 0)

    @pl.when(gz > 0)
    def _():
        greet((gx, gy, gz - 1))

    @pl.when(gz < n_gz - 1)
    def _():
        greet((gx, gy, gz + 1))

    part_sources(lambda dxi, cy, z, source: greet(source))

    pairs = (
        (tiles_in, tiles), (lists_in, lists), (shifts_in, shifts), (widths_in, widths), (backs_in, backs),
    )
    take = [pltpu.make_async_copy(a, b, local_sem.at[i]) for i, (a, b) in enumerate(pairs)]
    for copy in take:
        copy.start()

    halo[:, :, LIST_ROW:] = jnp.zeros((2, n, ROWS - LIST_ROW, LANES), jnp.bfloat16)
    if used < blocks * ROWS:
        got[:, used:] = jnp.zeros((n, blocks * ROWS - used, LANES), jnp.bfloat16)

    @pl.when(gz == 0)
    def _():
        halo[0, :, :LIST_ROW] = jnp.zeros((n, LIST_ROW, LANES), jnp.bfloat16)

    @pl.when(gz == n_gz - 1)
    def _():
        halo[1, :, :LIST_ROW] = jnp.zeros((n, LIST_ROW, LANES), jnp.bfloat16)

    for copy in take:
        copy.wait()
    flat = tiles[...].reshape(views * slots, depth)
    listed = (lists[...] + 1).astype(jnp.float32).astype(jnp.bfloat16)
    batch = min(n, 8)
    list_block, list_row = me // 32, LIST_ROW + me // 4 % 8
    for first in range(0, n, batch):
        shape = (batch * ROWS, views * slots)
        row = iota(shape, 0)
        q = row & (ROWS - 1)
        o = first + row // ROWS
        wanted = (q // CAPACITY) * slots + o * CAPACITY + (q & (CAPACITY - 1))
        pick = (iota(shape, 1) == wanted) & (q < views * CAPACITY)
        packed = dot(pick.astype(jnp.float32).astype(jnp.bfloat16), flat)
        shape = (slots, batch * LANES)
        lane = iota(shape, 1)
        spot = (first + lane // LANES) * CAPACITY + (lane & (CAPACITY - 1))
        spread = dot(listed, (iota(shape, 0) == spot).astype(jnp.float32).astype(jnp.bfloat16))
        lane = iota(spread.shape, 1) & (LANES - 1)
        mine = (lane // CAPACITY) == (me % 4) * (ROWS // CAPACITY) + iota(spread.shape, 0)
        ids = jnp.sum(jnp.where(mine, spread, 0.0), axis=0, keepdims=True)
        for i in range(batch):
            for b in range(blocks):
                body = packed[i * ROWS : (i + 1) * ROWS, b * LANES : (b + 1) * LANES]
                listing = (iota(body.shape, 0) == list_row) & (list_block == b)
                body = body + jnp.where(listing, ids[:, i * LANES : (i + 1) * LANES], 0.0)
                send[first + i, b * ROWS : (b + 1) * ROWS] = body.astype(jnp.bfloat16)
    got[me, :used] = send[me, :used]

    count = n - 1
    count = count + jnp.where(gz > 0, 1, 0) + jnp.where(gz < n_gz - 1, 1, 0)
    for dx in (-1, 0, 1):
        per = n_gz - (1 if dx == 0 else 0)
        per = per + jnp.where(in_y(gy + 1), 1, 0) + jnp.where(in_y(gy - 1), 1, 0)
        count = count + jnp.where(in_x(gx + dx), per, 0)
    pl.semaphore_wait(barrier, count)

    def send_tile(i, carry):
        o = (me + i) % n
        tile_copy(me, o, owner(o)).start()
        return carry

    lax.fori_loop(1, n, send_tile, 0)

    def pass_on(buf, src):
        @pl.when(gz > 0)
        def _():
            halo_copy(buf, src, 1, (gx, gy, gz - 1)).start()

        @pl.when(gz < n_gz - 1)
        def _():
            halo_copy(buf, src, 0, (gx, gy, gz + 1)).start()

    pass_on(send, me)

    step = (iota((LANES, LANES), 1) - iota((LANES, LANES), 0)).astype(jnp.float32)
    reach = iota((1, LANES), 1)
    span = views * LANES
    for b in range(blocks + 2):
        for d in range(blocks):
            if not 0 <= b - d <= 2:
                corr_w[b * span : (b + 1) * span, d * LANES : (d + 1) * LANES] = jnp.zeros((span, LANES), jnp.bfloat16)
    for v in range(views):
        shift = shifts[v].astype(jnp.float32)
        inv = 1.0 / jnp.full((1, LANES), widths[v], jnp.float32)
        curve = -0.5 * inv * inv
        far = reach.astype(jnp.float32)
        half = jnp.where((reach >= 1) & (reach <= PSF_REACH), jnp.exp(far * far * curve), 0.0)
        scale = 1.0 / (1.0 + 2.0 * jnp.sum(half, axis=1, keepdims=True))
        for m in range(3):
            for sign in (-1.0, 1.0):
                off = step - (m - 1.0) * LANES + sign * shift
                value = jnp.exp(off * off * curve) * scale
                value = jnp.where(jnp.abs(off) <= PSF_REACH, value, 0.0).astype(jnp.bfloat16)
                if sign < 0:
                    blur_w[m * LANES : (m + 1) * LANES, v * LANES : (v + 1) * LANES] = value
                    continue
                for d in range(blocks):
                    at = (d + m) * span + v * LANES
                    corr_w[at : at + LANES, d * LANES : (d + 1) * LANES] = value

    half_depth = depth // 2
    z = iota((depth, half_depth + LANES), 0)
    k = iota((depth, half_depth + LANES), 1)
    k = jnp.where(k == half_depth + LANES - 1, -1, k)
    thin[...] = tap(z - 2 * k + 1).astype(jnp.bfloat16)
    r = iota((8, lines), 0)
    column = iota((8, lines), 1)

    def weight_of(dx, t, i, j):
        dy, z_part = (0, t) if t < n_gz else ((1, 0) if t == n_gz else (-1, n_gz - 1))
        i = rows_x * dx + i
        j = (CY // 2) * dy + rows_y * z_part + j
        return tap(column // CY - 2 * i + 1) * tap(column % CY - 2 * j + 1)

    rows = [
        jnp.where(r < rows_x * rows_y, weight_of(0, t, r // rows_y, r % rows_y), 0.0) for t in range(group)
    ]
    for first in range(0, 2 * group * rows_y, 8):
        block = jnp.zeros((8, lines), jnp.float32)
        for e in range(2 * group):
            for j in range(rows_y):
                at = e * rows_y + j - first
                if 0 <= at < 8:
                    dx, i = (-1, rows_x - 1) if e < group else (1, 0)
                    block = jnp.where(r == at, weight_of(dx, e % group, i, j), block)
        rows.append(block)
    weights[...] = jnp.concatenate(rows, axis=0).astype(jnp.bfloat16)

    def take_tile(i, carry):
        src = (me + n - i) % n
        tile_copy(src, me, owner(src)).wait_recv()
        pass_on(got, src)
        return carry

    lax.fori_loop(1, n, take_tile, 0)

    total = None
    for b in range(blocks if used == blocks * ROWS else 1):
        at = b * ROWS + 16
        ids = got[0, at : at + 16].astype(jnp.float32)
        for src in range(1, n):
            ids = ids + got[src, at : at + 16].astype(jnp.float32)
        total = ids[8:] if total is None else jnp.concatenate([total, ids[8:]], axis=0)
    ids = total
    line = (iota((lines, batch * ROWS), 0) + 1).astype(jnp.float32)
    lane = iota((lines, batch * ROWS), 1)
    view = (lane // CAPACITY) & (ROWS // CAPACITY - 1)

    for first in range(0, n, batch):
        at = first // 4
        pieces = [ids[at + i : at + i + 1] for i in range(-(-batch // 4))]
        hit = jnp.concatenate(pieces, axis=1)[:, : batch * ROWS] == line
        for v in range(views):
            owned = jnp.where(hit & (view == v), 1.0, 0.0)
            members[first // batch, v * lines : (v + 1) * lines] = owned.astype(jnp.bfloat16)
        owned = jnp.where(hit & (view < views), 1.0, 0.0)
        members[first // batch, views * lines :] = owned.astype(jnp.bfloat16)

    def landed(rows, load):
        total = None
        for first in range(0, n, batch):
            term = dot(members[first // batch, rows], load(first))
            total = term if total is None else total + term
        return total

    every = slice(0, views * lines)
    merged = slice(views * lines, (views + 1) * lines)

    def own(first):
        return jnp.concatenate(
            [
                got[first : first + batch, b * ROWS : (b + 1) * ROWS].reshape(batch * ROWS, LANES)
                for b in range(blocks)
            ],
            axis=1,
        )

    def beside(first):
        return jnp.concatenate(
            [halo[side, first : first + batch].reshape(batch * ROWS, LANES) for side in range(2)], axis=1
        )

    est = landed(merged, own) / views
    est_b[...] = est.astype(jnp.bfloat16)
    vd[...] = landed(every, own)
    for b in range(blocks + 2):
        low, high = max(b - 1, 1), min(b + 2, blocks + 1)
        partial[:, b * span : (b + 1) * span] = dot(
            est_b[:, (low - 1) * LANES : (high - 1) * LANES],
            blur_w[(low - b + 1) * LANES : (high - b + 1) * LANES],
        )

    def ratio_of(b, blurred):
        for v in range(views):
            rows = slice(v * lines, (v + 1) * lines)
            if b == 0:
                data = vd_side[rows, :LANES]
            elif b == blocks + 1:
                data = vd_side[rows, LANES:]
            else:
                data = vd[rows, (b - 1) * LANES : b * LANES]
            value = data / (blurred[:, v * LANES : (v + 1) * LANES] + jnp.full((1, LANES), backs[v], jnp.float32))
            ratio[:, b * span + v * LANES : b * span + (v + 1) * LANES] = value.astype(jnp.bfloat16)

    for b in range(2, blocks):
        ratio_of(b, partial[:, b * span : (b + 1) * span])

    @pl.when(gz > 0)
    def _():
        for src in range(n):
            halo_copy(got, src, 0, (gx, gy, gz)).wait_recv()

    @pl.when(gz < n_gz - 1)
    def _():
        for src in range(n):
            halo_copy(got, src, 1, (gx, gy, gz)).wait_recv()

    side = (landed(merged, beside) / views).astype(jnp.bfloat16)
    vd_side[...] = landed(every, beside)
    for edge, near, m, column_block in ((0, 1, 0, 0), (blocks + 1, blocks, 2, 1)):
        here = side[:, column_block * LANES : (column_block + 1) * LANES]
        for b, w in ((edge, 1), (near, m)):
            blurred = partial[:, b * span : (b + 1) * span] + dot(here, blur_w[w * LANES : (w + 1) * LANES])
            if blocks == 1 and b == 1:
                partial[:, span : 2 * span] = blurred
            ratio_of(b, blurred)
    correction = dot(ratio[...], corr_w[...])
    joined = est * (correction / views)
    joined_out[...] = joined.reshape(CX, CY, depth)

    halved = dot_split(joined, thin[...]) * (1.0 / 8)
    high = halved.astype(jnp.bfloat16)
    low = (halved - high.astype(jnp.float32)).astype(jnp.bfloat16)
    shares = (dot(weights[...], high) + dot(weights[...], low)) * (1.0 / 64)
    parts[...] = shares[: group * 8].reshape(group, 8, half_depth + LANES)
    for e in range(2 * group):
        at = group * 8 + e * rows_y
        edges[e // group, e % group] = shares[at : at + rows_y]
    part_sends(lambda dxi, part, cy, target: part_copy(dxi, part, cy, gz, target).start())
    sums[1, gz] = parts[gz]
    def sent_tile(i, carry):
        o = (me + i) % n
        tile_copy(me, o, owner(o)).wait_send()
        return carry

    lax.fori_loop(1, n, sent_tile, 0)

    @pl.when(gz > 0)
    def _():
        for src in range(n):
            halo_copy(got, src, 1, (gx, gy, gz)).wait_send()

    @pl.when(gz < n_gz - 1)
    def _():
        for src in range(n):
            halo_copy(got, src, 0, (gx, gy, gz)).wait_send()

    part_sources(lambda dxi, cy, s, source: part_copy(dxi, 0, cy, s, source).wait_recv())
    totals = []
    for s in range(n_gz):
        total = sums[1, s]
        above, below = in_y(gy + 1) & (gz == n_gz - 1), in_y(gy - 1) & (gz == 0)
        total = total + jnp.where(above, sums[0, s], 0.0) + jnp.where(below, sums[2, s], 0.0)
        sides = []
        for index, dx in ((1, 1), (0, -1)):
            side = edge_sums[index, 1, s]
            side = side + jnp.where(above, edge_sums[index, 0, s], 0.0) + jnp.where(below, edge_sums[index, 2, s], 0.0)
            sides.append(jnp.where(in_x(gx - dx), side, 0.0))
        sides.insert(1, jnp.zeros(((rows_x - 2) * rows_y, half_depth + LANES), jnp.float32))
        if rows_x * rows_y < 8:
            sides.append(jnp.zeros((8 - rows_x * rows_y, half_depth + LANES), jnp.float32))
        total = total + jnp.concatenate(sides, axis=0)
        totals.append(total)
    lane = iota((8, half_depth), 1)
    for s in range(n_gz):
        total = totals[s][:, :half_depth]
        if s > 0:
            after = totals[s - 1][:, half_depth : half_depth + LANES]
            total = total + jnp.where(lane == 0, spread_lanes(after, half_depth), 0.0)
        if s < n_gz - 1:
            before = totals[s + 1][:, half_depth : half_depth + LANES]
            total = total + jnp.where(lane == half_depth - 1, spread_lanes(before, half_depth), 0.0)
        for i in range(rows_x):
            coarse_out[i, :, s * half_depth : (s + 1) * half_depth] = total[i * rows_y : (i + 1) * rows_y]
    part_sends(lambda dxi, part, cy, target: part_copy(dxi, part, cy, gz, target).wait_send())


def hand_on(joined, coarse, joined_out, coarse_out, sem):
    pairs = ((joined, joined_out), (coarse, coarse_out))
    put = [pltpu.make_async_copy(a, b, sem.at[i]) for i, (a, b) in enumerate(pairs)]
    for copy in put:
        copy.start()
    for copy in put:
        copy.wait()


def on_device(n_gx, n_gy, n_gz, camera_tiles, slot_lines, view_shifts, psf_width, background):
    views, slots, depth = camera_tiles.shape
    n = n_gx * n_gy
    group = n_gz + 2
    packets = 3 * group
    rows_y = CY // 2 // n_gz
    blocks = depth // LANES
    lines = CX * CY
    span = views * LANES
    vmem = pl.BlockSpec(memory_space=pltpu.VMEM)
    hbm = pl.BlockSpec(memory_space=pl.ANY)
    results = pl.pallas_call(
        functools.partial(kernel, n_gx, n_gy, n_gz),
        out_shape=(
            pltpu.VMEM((CX, CY, depth), jnp.float32),
            pltpu.VMEM((CX // 2, CY // 2 // n_gz, depth // 2 * n_gz), jnp.float32),
        ),
        in_specs=[hbm] * 5,
        out_specs=(vmem, vmem),
        scratch_shapes=[
            pltpu.SMEM((views,), jnp.int32),
            pltpu.SMEM((views,), jnp.float32),
            pltpu.SMEM((views,), jnp.float32),
            pltpu.VMEM((views, slots, depth), jnp.bfloat16),
            pltpu.VMEM((views, slots), jnp.int32),
            pltpu.SemaphoreType.DMA((5,)),
            pltpu.VMEM((depth, depth // 2 + LANES), jnp.bfloat16),
            pltpu.VMEM((group * 8 + -(-2 * group * rows_y // 8) * 8, lines), jnp.bfloat16),
            pltpu.VMEM((-(-n // 8), (views + 1) * lines, min(n, 8) * ROWS), jnp.bfloat16),
            pltpu.VMEM((n, blocks * ROWS, LANES), jnp.bfloat16),
            pltpu.VMEM((n, blocks * ROWS, LANES), jnp.bfloat16),
            pltpu.VMEM((2, n, ROWS, LANES), jnp.bfloat16),
            pltpu.VMEM((views * lines, depth), jnp.float32),
            pltpu.VMEM((views * lines, 2 * LANES), jnp.float32),
            pltpu.VMEM((lines, depth), jnp.bfloat16),
            pltpu.VMEM((lines, (blocks + 2) * span), jnp.float32),
            pltpu.VMEM((lines, (blocks + 2) * span), jnp.bfloat16),
            pltpu.VMEM((3 * LANES, span), jnp.bfloat16),
            pltpu.VMEM(((blocks + 2) * span, depth), jnp.bfloat16),
            pltpu.VMEM((group, 8, depth // 2 + LANES), jnp.float32),
            pltpu.VMEM((2, group, rows_y, depth // 2 + LANES), jnp.float32),
            pltpu.VMEM((3, n_gz, 8, depth // 2 + LANES), jnp.float32),
            pltpu.VMEM((2, 3, n_gz, rows_y, depth // 2 + LANES), jnp.float32),
            pltpu.SemaphoreType.DMA((n,)),
            pltpu.SemaphoreType.DMA((n,)),
            pltpu.SemaphoreType.DMA((2, n)),
            pltpu.SemaphoreType.DMA((2, n)),
            pltpu.SemaphoreType.DMA((packets,)),
            pltpu.SemaphoreType.DMA((9, n_gz)),
        ],
        compiler_params=pltpu.CompilerParams(collective_id=0, has_side_effects=True),
    )(view_shifts, psf_width, background, camera_tiles, slot_lines)
    return pl.pallas_call(
        hand_on,
        out_shape=tuple(jax.ShapeDtypeStruct(r.shape, r.dtype) for r in results),
        in_specs=[vmem, vmem],
        out_specs=(hbm, hbm),
        scratch_shapes=[pltpu.SemaphoreType.DMA((2,))],
        compiler_params=pltpu.CompilerParams(has_side_effects=True),
    )(*[pltpu.with_memory_space_constraint(r, pltpu.VMEM) for r in results])


def solution(mesh):
    sizes = (mesh.shape["gx"], mesh.shape["gy"], mesh.shape["gz"])
    in_specs = (P(None, ("gx", "gy"), "gz"), P(None, ("gx", "gy")), P(), P(), P())
    out_specs = (P("gx", "gy", "gz"), P("gx", ("gy", "gz"), None))
    return jax.shard_map(
        functools.partial(on_device, *sizes), mesh=mesh, in_specs=in_specs, out_specs=out_specs,
        check_vma=False,
    )
```
